256 devices in a mesh: grp: 4 (over z_lo), dp: 64 (over z_hi, x, y, core).
Axes of the slice: x: 4, y: 4, z: 8 (z_hi: 2, z_lo: 4; z = z_hi * 4 + z_lo), core: 2. Of those that a mesh axis runs over, the one named last changes fastest.
Arguments:
- grads: bfloat16 [4, 64, 64, 8192], P('grp', 'dp'), may hold values from -12 to 12
- momentum: float32 [4, 64, 64, 8192], P('grp', 'dp'), may hold values from -152 to 152
- worker_error: float32 [4, 64, 64, 8192], P('grp', 'dp'), may hold values from -6 to 6
- server_error: float32 [4, 64, 8192], P('grp', 'dp'), may hold values from -2 to 2
Outputs:
- synced: float32 [64, 8192], replicated
- worker_error_out: float32 [4, 64, 64, 8192], P('grp', 'dp')
- server_error_out: float32 [4, 64, 8192], P('grp', 'dp')
The draws below stay inside these ranges and needn't reach their ends.
All inputs are finite; a program needn't handle non-finite values.
Results may differ from the reference program's by a relative error of at most 0.012.
Values may be sent and summed in bfloat16 or wider, within the bound.
No kernel may reach another device: no remote copies, remote signals or barrier semaphores. Data moves between devices by JAX's collectives and lax.ppermute only.
A program may use at most 64 MiB of HBM per device.

```python
import math
import jax
import jax.numpy as jnp
from jax import lax

D = 8192
GROUPS = 4
WORKERS = 64
BUCKET_ROWS = 64


def draw_momentum(key, part):
    key_noise, key_rows, key_cols = jax.random.split(key, 3)
    row_factor = jnp.exp(jax.random.uniform(key_rows, (BUCKET_ROWS, 1), jnp.float32, math.log(0.3), math.log(3.0)))
    col_factor = jnp.exp(jax.random.uniform(key_cols, (1, D), jnp.float32, math.log(0.3), math.log(3.0)))
    noise = jnp.clip(jax.random.normal(key_noise, (GROUPS, WORKERS, BUCKET_ROWS, D), jnp.float32), -6.0, 6.0)
    return 2.0 * noise * row_factor * col_factor


def steps_of(rng, shape, cuts, low, high):
    def one(position, blocks):
        heights = jax.random.uniform(jax.random.fold_in(jax.random.fold_in(rng, 6), position), (blocks,), jnp.float32, low / len(cuts), high / len(cuts))
        return jnp.repeat(jnp.exp(heights), shape[position] // blocks).reshape((-1,) + (1,) * (len(shape) - position - 1))

    level = one(*cuts[0])
    for cut in cuts[1:]:
        level = level * one(*cut)
    return level


def normal_values(stream_key, dims, spread, reach, cuts=(), kind=jnp.bfloat16):
    entries = spread * jax.random.normal(stream_key, dims, jnp.float32)
    if cuts:
        entries = entries * steps_of(stream_key, dims, cuts, -0.22, 0.18)
    return jnp.clip(entries, -reach, reach).astype(kind)


def setup_inputs(seed: int = 0) -> dict:
    arg_keys = jax.random.split(jax.random.key(seed), 5)
    grads = normal_values(arg_keys[0], (GROUPS, WORKERS, BUCKET_ROWS, D), 2.0, 12.0, ((0, 4), (1, 64)))
    momentum = draw_momentum(jax.random.fold_in(arg_keys[4], 71), 0)
    worker_error = normal_values(arg_keys[2], (GROUPS, WORKERS, BUCKET_ROWS, D), 1.0, 6.0, ((0, 4), (1, 64)), jnp.float32)
    server_error = normal_values(arg_keys[3], (GROUPS, BUCKET_ROWS, D), 0.3, 2.0, ((0, 4), (1, 64)), jnp.float32)
    return {"grads": grads, "momentum": momentum, "worker_error": worker_error, "server_error": server_error}


def compress(values):
    row_scale = (jnp.mean(jnp.abs(values), axis=-1, keepdims=True) + 1e-6).astype(jnp.bfloat16)
    scale_wide = row_scale.astype(jnp.float32)
    coded = jnp.tanh(values / scale_wide).astype(jnp.bfloat16)
    leftover = values - scale_wide * coded.astype(jnp.float32)
    return row_scale, coded, leftover


def one_group(packed):
    grad_part, moment_part, werr_part, serr_part = packed
    blended = 0.9 * moment_part + 0.1 * grad_part.astype(jnp.float32) + werr_part
    row_scale, coded, werr_new = compress(blended)
    summed = jnp.einsum("wrd,wr->rd", coded.astype(jnp.float32), row_scale[..., 0].astype(jnp.float32))
    server_input = summed / WORKERS + serr_part
    server_scale, server_code, serr_new = compress(server_input)
    decoded = server_scale.astype(jnp.float32) * server_code.astype(jnp.float32)
    return werr_new, serr_new, decoded


def reference(grads, momentum, worker_error, server_error):
    werr_all, serr_all, decoded_all = lax.map(one_group, (grads, momentum, worker_error, server_error))
    synced = jnp.sum(decoded_all, axis=0) / GROUPS
    return synced, werr_all, serr_all
```

```python
import functools

import jax
import jax.numpy as jnp
from jax import lax
from jax.experimental import pallas as pl
from jax.experimental.pallas import tpu as pltpu
from jax.sharding import Mesh
from jax.sharding import PartitionSpec as P

DP = ("zh", "x", "y", "core")
F32, BF16 = jnp.float32, jnp.bfloat16
LANES, SUB = 128, 8
EPS = 1e-6


def blend(m, g, e):
    return 0.9 * m + 0.1 * g.astype(F32) + e


def row_scale(total, width):
    return (total * (1.0 / width) + EPS).astype(BF16).astype(F32)


def encode_kernel(core_ref, g_ref, m_ref, e_ref, theirs_ref, mine_ref, scale_ref, tile):
    width = m_ref.shape[1]
    cols = width // LANES
    total = jnp.zeros((SUB, LANES), F32)
    for j in range(cols):
        at = pl.ds(j * LANES, LANES)
        b = blend(m_ref[:, at], g_ref[:, at], e_ref[:, at])
        tile[pl.ds(j * SUB, SUB), :] = b
        total = total + jnp.abs(b)
    scale = row_scale(jnp.sum(total, axis=1, keepdims=True), width)
    wide = jnp.broadcast_to(scale, (SUB, LANES))
    inverse = jnp.broadcast_to(1.0 / scale, (SUB, LANES))
    scale_ref[...] = wide
    for j in range(cols):
        at = pl.ds(j * SUB, SUB)
        code = jnp.tanh(tile[at, :] * inverse).astype(BF16).astype(F32)
        tile[at, :] = wide * code
    core = core_ref[0]
    for i in range(SUB // 2):
        for q in range(cols // SUB):
            to = pl.ds(q * SUB, SUB)
            base = q * SUB * SUB + 2 * i
            mine_ref[i, to, :] = tile[pl.ds(base + core, SUB, stride=SUB), :]
            theirs_ref[i, to, :] = tile[pl.ds(base + 1 - core, SUB, stride=SUB), :].astype(BF16)


def encode(core, g, m, e):
    rows, width = m.shape
    cols = width // LANES
    block = pl.BlockSpec((SUB, width), lambda i, c: (i, 0))
    half = pl.BlockSpec((SUB // 2, cols, LANES), lambda i, c: (i, 0, 0))
    return pl.pallas_call(
        encode_kernel,
        grid_spec=pltpu.PrefetchScalarGridSpec(
            num_scalar_prefetch=1,
            grid=(rows // SUB,),
            in_specs=[block, block, block],
            out_specs=[half, half, pl.BlockSpec((SUB, LANES), lambda i, c: (i, 0))],
            scratch_shapes=[pltpu.VMEM((cols * SUB, LANES), F32)],
        ),
        out_shape=[
            jax.ShapeDtypeStruct((rows // 2, cols, LANES), BF16),
            jax.ShapeDtypeStruct((rows // 2, cols, LANES), F32),
            jax.ShapeDtypeStruct((rows, LANES), F32),
        ],
        name="encode",
    )(core, g, m, e)


def leftover_kernel(g_ref, m_ref, e_ref, scale_ref, out_ref):
    wide = scale_ref[...]
    inverse = 1.0 / wide
    for j in range(m_ref.shape[1] // LANES):
        at = pl.ds(j * LANES, LANES)
        b = blend(m_ref[:, at], g_ref[:, at], e_ref[:, at])
        code = jnp.tanh(b * inverse).astype(BF16).astype(F32)
        out_ref[:, at] = b - wide * code


def leftover(g, m, e, scale):
    rows, width = m.shape
    block = pl.BlockSpec((SUB, width), lambda i: (i, 0))
    return pl.pallas_call(
        leftover_kernel,
        grid=(rows // SUB,),
        in_specs=[block, block, block, pl.BlockSpec((SUB, LANES), lambda i: (i, 0))],
        out_specs=block,
        out_shape=jax.ShapeDtypeStruct((rows, width), F32),
        name="leftover",
    )(g, m, e, scale)


def pair_kernel(a_ref, b_ref, out_ref):
    out_ref[...] = (a_ref[...] + b_ref[...].astype(F32)).astype(BF16)


def pair_sum(a, b):
    return pl.pallas_call(
        pair_kernel, out_shape=jax.ShapeDtypeStruct(a.shape, BF16), name="pair_sum"
    )(a, b)


def server_kernel(workers, got_ref, e_ref, copies_ref, out_ref):
    total = got_ref[0].astype(F32)
    for k in range(1, got_ref.shape[0]):
        total = total + got_ref[k].astype(F32)
    x = total * (1.0 / workers) + e_ref[...]
    scale = row_scale(jnp.sum(jnp.abs(x), keepdims=True), x.size)
    code = jnp.tanh(x / scale).astype(BF16).astype(F32)
    decoded = scale * code
    out_ref[...] = x - decoded
    sent = decoded.astype(BF16)
    for k in range(copies_ref.shape[0]):
        copies_ref[k] = sent


def server(got, e, workers, copies):
    return pl.pallas_call(
        functools.partial(server_kernel, workers),
        out_shape=[
            jax.ShapeDtypeStruct((copies, *e.shape), BF16),
            jax.ShapeDtypeStruct(e.shape, F32),
        ],
        name="server",
    )(got, e)


def average_kernel(got_ref, out_ref):
    groups, halves = got_ref.shape[0], got_ref.shape[1]
    for h in range(halves):
        total = got_ref[0, h].astype(F32)
        for k in range(1, groups):
            total = total + got_ref[k, h].astype(F32)
        sent = (total * (1.0 / groups)).astype(BF16)
        for k in range(out_ref.shape[0]):
            out_ref[k, h] = sent


def average(got, copies):
    return pl.pallas_call(
        average_kernel,
        out_shape=jax.ShapeDtypeStruct((copies, *got.shape[1:]), BF16),
        name="average",
    )(got)


def assemble_kernel(core_ref, mine_ref, theirs_ref, out_ref, tile):
    core = core_ref[0]
    cols = out_ref.shape[1] // LANES
    for i in range(SUB // 2):
        for q in range(cols // SUB):
            at = pl.ds(q * SUB, SUB)
            base = q * SUB * SUB + 2 * i
            tile[pl.ds(base + core, SUB, stride=SUB), :] = mine_ref[0, i, 0, at, :].astype(F32)
            tile[pl.ds(base + 1 - core, SUB, stride=SUB), :] = theirs_ref[0, i, 0, at, :].astype(F32)
    for j in range(cols):
        out_ref[:, pl.ds(j * LANES, LANES)] = tile[pl.ds(j * SUB, SUB), :]


def assemble(core, mine, theirs):
    xs, ys, zs, cols, _ = mine.shape
    assert ys * 2 == SUB
    rows, width = xs * ys * zs * 2, cols * LANES
    part = pl.BlockSpec((1, ys, 1, cols, LANES), lambda i, c: (i % xs, 0, i // xs, 0, 0))
    return pl.pallas_call(
        assemble_kernel,
        grid_spec=pltpu.PrefetchScalarGridSpec(
            num_scalar_prefetch=1,
            grid=(rows // SUB,),
            in_specs=[part, part],
            out_specs=pl.BlockSpec((SUB, width), lambda i, c: (i, 0)),
            scratch_shapes=[pltpu.VMEM((cols * SUB, LANES), F32)],
        ),
        out_shape=jax.ShapeDtypeStruct((rows, width), F32),
        name="assemble",
    )(core, mine, theirs)


def everyone(x, axes):
    return lax.all_to_all(x, axes, split_axis=0, concat_axis=0, tiled=True)


def swapped(x):
    return lax.ppermute(x, "core", [(0, 1), (1, 0)])


def per_device(grads, momentum, worker_error, server_error):
    g, m, e = (a[0, 0] for a in (grads, momentum, worker_error))
    width = m.shape[1]
    cols = width // LANES
    zs, xs, ys = (lax.axis_size(n) for n in ("zh", "x", "y"))
    groups, workers = lax.axis_size("grp"), lax.axis_size(DP)
    core = lax.axis_index("core").astype(jnp.int32)[None]
    theirs, mine, scale = encode(core, g, m, e)
    partial = pair_sum(mine, swapped(theirs))
    got = everyone(partial, ("zh", "x", "y"))
    werr = leftover(g, m, e, scale)
    copies, serr = server(got, server_error.reshape(cols, LANES), workers, groups * zs)
    rows = everyone(copies, ("grp", "zh")).reshape(groups, zs, cols, LANES)
    spread = average(rows, xs * ys)
    own = everyone(spread, ("x", "y")).reshape(xs, ys, zs, cols, LANES)
    synced = assemble(core, own, swapped(own))
    return (synced, werr[None, None], serr.reshape(1, 1, width))


def solution(mesh):
    torus = Mesh(
        mesh.devices.reshape(mesh.shape["grp"], 2, 4, 4, 2), ("grp", "zh", "x", "y", "core")
    )
    return jax.shard_map(
        per_device,
        mesh=torus,
        in_specs=(
            P("grp", DP, None, None),
            P("grp", DP, None, None),
            P("grp", DP, None, None),
            P("grp", DP, None),
        ),
        out_specs=(P(), P("grp", DP, None, None), P("grp", DP, None)),
        check_vma=False,
    )
```
